32 devices in a mesh: rows: 8 (over z, x), strips: 4 (over y, core).
Axes of the slice: x: 2, y: 2, z: 4, core: 2. Of those that a mesh axis runs over, the one named last changes fastest.
Arguments:
- tokens: bfloat16 [8, 24, 64, 1280], P('rows', None, 'strips'), may hold values from -8 to 8
- stale_kv: bfloat16 [8, 2, 1536, 1280], P('rows', None, 'strips'), may hold values from -180 to 180
- stale_moments: float32 [8, 4, 2, 32], P('rows', 'strips'), as said below
- norm_gain: float32 [1280], replicated, may hold values from 0.1 to 1.9
- norm_bias: float32 [1280], replicated, may hold values from -3 to 3
- w_query: bfloat16 [1280, 1280], P('rows'), may hold values from -0.33398438 to 0.33398438
- w_key: bfloat16 [1280, 1280], P('rows'), may hold values from -0.1953125 to 0.1953125
- w_value: bfloat16 [1280, 1280], P('rows'), may hold values from -0.15625 to 0.15625
- w_out: bfloat16 [1280, 1280], P('rows'), may hold values from -0.33398438 to 0.33398438
Outputs:
- attended: bfloat16 [8, 24, 64, 1280], P('rows', None, 'strips')
- fresh_kv: bfloat16 [8, 2, 1536, 1280], P('rows', None, 'strips')
- fresh_sums: float32 [8, 4, 32], P('rows', 'strips')
- fresh_squares: float32 [8, 4, 32], P('rows', 'strips')
The draws below stay inside these ranges and needn't reach their ends.
Inputs may be any that keep to these rules, and one draw needn't show every extreme that they name: `stale_moments`: each strip's entries are a sum of 15360 values and the sum of their squares.
All inputs are finite; a program needn't handle non-finite values.
Results may differ from the reference program's by a relative error of at most 0.0075.
The reference program's roundings to bfloat16 on the way (of `normed` and `heads_out`) count: a program that leaves them out, or rounds other values in their place, can miss the bound.
Values may be sent and summed in bfloat16 or wider, within the bound.
No kernel may reach another device: no remote copies, remote signals or barrier semaphores. Data moves between devices by JAX's collectives and lax.ppermute only.
A program may use at most 128 MiB of HBM per device.

```python
import jax
import jax.numpy as jnp
from jax import lax

C = 1280
GROUPS = 32
HEADS = 20
HEAD = 64
ROWS_IMG = 24
SW = 16
CG = 40
HD = 1280
TOK_DEV = 384
GRID_COLS = 64
KEYS = 1536
IMAGES = 8
N_STRIPS = 4


def draw_stale_kv(key, part):
    first = jax.random.fold_in(key, 0)
    base = jnp.clip(jax.random.normal(first, (IMAGES, 2, KEYS, HD), jnp.float32), -6.0, 6.0)
    return base.astype(jnp.bfloat16)


def draw_stale_moments(key, part):
    first, second = jax.random.split(key)
    count = float(TOK_DEV * CG)
    index = jnp.arange(N_STRIPS, dtype=jnp.float32)[None, :, None]
    rising = 1.0 + 2.0 * index / max(N_STRIPS - 1, 1)
    mean = 0.3 * jax.random.normal(first, (IMAGES, N_STRIPS, GROUPS), jnp.float32)
    var = jnp.exp(jax.random.uniform(second, (IMAGES, N_STRIPS, GROUPS), jnp.float32, -0.5, 0.35)) * rising
    return jnp.stack([count * mean, count * (var + mean * mean)], axis=2).astype(jnp.float32)


def shard_levels(stream_key, extent, pieces, least, largest):
    factor_of = 1.0
    for axis_at, parts in pieces:
        heights = jax.random.uniform(jax.random.fold_in(jax.random.fold_in(stream_key, 6), axis_at), (parts,), jnp.float32, least / len(pieces), largest / len(pieces))
        factor_of = factor_of * jnp.repeat(jnp.exp(heights), extent[axis_at] // parts).reshape((-1,) + (1,) * (len(extent) - 1 - axis_at))
    return factor_of


def normal_values(stream_key, shape, deviation, limit, pieces=(), kind=jnp.bfloat16):
    factor_of = shard_levels(stream_key, shape, pieces, -0.22, 0.18) if pieces else 1.0
    entries = jax.random.normal(stream_key, shape, jnp.float32) * deviation * factor_of
    return jnp.minimum(jnp.maximum(entries, -limit), limit).astype(kind)


def setup_inputs(seed: int = 0) -> dict:
    keys = jax.random.split(jax.random.key(seed), 10)
    tokens = normal_values(keys[0], (IMAGES, ROWS_IMG, GRID_COLS, C), 1.3, 8.0, ((0, 8), (2, 4)))
    stale_kv = draw_stale_kv(jax.random.fold_in(keys[9], 71), 0)
    stale_moments = draw_stale_moments(jax.random.fold_in(keys[9], 71), 0)
    norm_gain = jnp.clip(1.0 + 0.18 * jax.random.normal(keys[3], (C,), jnp.float32), 0.1, 1.9)
    norm_bias = normal_values(keys[4], (C,), 0.5, 3.0, (), jnp.float32)
    w_query = normal_values(keys[5], (C, HD), (2.0 / C ** 0.5), 0.33398438, ((0, 8),))
    w_key = normal_values(keys[6], (C, HD), (1.15 / C ** 0.5), 0.1953125, ((0, 8),))
    w_value = normal_values(keys[7], (C, HD), C ** -0.5, 0.15625, ((0, 8),))
    w_out = normal_values(keys[8], (HD, C), (2.0 / HD ** 0.5), 0.33398438, ((0, 8),))
    return dict(tokens=tokens, stale_kv=stale_kv, stale_moments=stale_moments, norm_gain=norm_gain, norm_bias=norm_bias, w_query=w_query, w_key=w_key, w_value=w_value, w_out=w_out)


def reference(tokens, stale_kv, stale_moments, norm_gain, norm_bias, w_query, w_key, w_value, w_out):
    count = float(KEYS * CG)
    positions = jnp.arange(KEYS, dtype=jnp.int32)
    highest = lax.Precision.HIGHEST

    def one_image(items):
        image, kv_old, moments_old = items
        blocks = image.reshape(ROWS_IMG, N_STRIPS, SW, C).transpose(1, 0, 2, 3).reshape(N_STRIPS, TOK_DEV, C).astype(jnp.float32)
        grouped = blocks.reshape(N_STRIPS, TOK_DEV, GROUPS, CG)
        fresh = jnp.stack([grouped.sum(axis=(1, 3)), (grouped * grouped).sum(axis=(1, 3))], axis=1)
        mixed = lax.optimization_barrier(jnp.sum(moments_old, axis=0))[None] - moments_old + fresh
        mean = mixed[:, 0] / count
        var = mixed[:, 1] / count - mean * mean
        rstd = lax.rsqrt(var + 1e-05)
        normed = ((grouped - mean[:, None, :, None]) * rstd[:, None, :, None]).reshape(N_STRIPS, TOK_DEV, C)
        normed = (normed * norm_gain + norm_bias).astype(jnp.bfloat16).reshape(KEYS, C)
        query = (jnp.dot(normed, w_query, preferred_element_type=jnp.float32) * (1.0 / HEAD ** 0.5)).astype(jnp.bfloat16)
        key = jnp.dot(normed, w_key, preferred_element_type=jnp.float32).astype(jnp.bfloat16)
        value = jnp.dot(normed, w_value, preferred_element_type=jnp.float32).astype(jnp.bfloat16)
        far_keys = kv_old[0].astype(jnp.float32).reshape(KEYS, HEADS, HEAD)
        far_vals = kv_old[1].astype(jnp.float32).reshape(KEYS, HEADS, HEAD)

        def one_strip(strip):
            start = (strip * TOK_DEV).astype(jnp.int32)
            qry = lax.dynamic_slice_in_dim(query, start, TOK_DEV, 0).astype(jnp.float32).reshape(TOK_DEV, HEADS, HEAD)
            near_k = lax.dynamic_slice_in_dim(key, start, TOK_DEV, 0).astype(jnp.float32).reshape(TOK_DEV, HEADS, HEAD)
            near_v = lax.dynamic_slice_in_dim(value, start, TOK_DEV, 0).astype(jnp.float32).reshape(TOK_DEV, HEADS, HEAD)
            far_s = jnp.einsum('qhe,khe->hqk', qry, far_keys, precision=highest)
            inside = (positions >= start) & (positions < start + TOK_DEV)
            far_s = jnp.where(inside[None, None, :], jnp.float32(-1e+30), far_s)
            near_s = jnp.einsum('qhe,khe->hqk', qry, near_k, precision=highest)
            top = jnp.maximum(far_s.max(axis=-1), near_s.max(axis=-1))
            far_p = jnp.exp(far_s - top[..., None])
            near_p = jnp.exp(near_s - top[..., None])
            total = far_p.sum(axis=-1) + near_p.sum(axis=-1)
            weighted = jnp.einsum('hqk,khe->hqe', far_p, far_vals, precision=highest) + jnp.einsum('hqk,khe->hqe', near_p, near_v, precision=highest)
            heads_out = (weighted / total[..., None]).transpose(1, 0, 2).reshape(TOK_DEV, HD).astype(jnp.bfloat16)
            return jnp.dot(heads_out, w_out, preferred_element_type=jnp.float32).astype(jnp.bfloat16)
        outs = lax.map(one_strip, jnp.arange(N_STRIPS, dtype=jnp.int32))
        attended = outs.reshape(N_STRIPS, ROWS_IMG, SW, C).transpose(1, 0, 2, 3).reshape(ROWS_IMG, GRID_COLS, C)
        return (attended, jnp.stack([key, value]), fresh[:, 0], fresh[:, 1])
    attended, fresh_kv, fresh_sums, fresh_squares = lax.map(one_image, (tokens, stale_kv, stale_moments))
    return (attended, fresh_kv, fresh_sums, fresh_squares)
```

```python
import functools

import jax
import jax.numpy as jnp
from jax import lax
from jax.experimental import pallas as pl
from jax.experimental.pallas import tpu as pltpu
from jax.sharding import PartitionSpec as P

HEAD = 64
PAIR = 2 * HEAD
EPS = 1e-05


def group_matrix(chans, groups):
    per = chans // groups
    first = lax.broadcasted_iota(jnp.int32, (chans, groups), 1) * per
    place = lax.broadcasted_iota(jnp.int32, (chans, groups), 0)
    return jnp.where((place >= first) & (place < first + per), 1.0, 0.0).astype(jnp.float32)


def norm_kernel(count, tok_ref, other_ref, gain_ref, bias_ref, fresh_ref, out_ref):
    chans = tok_ref.shape[1]
    groups = fresh_ref.shape[1]
    values = tok_ref[...].astype(jnp.float32)
    sums = jnp.sum(values, axis=0, keepdims=True)
    squares = jnp.sum(values * values, axis=0, keepdims=True)
    row = lax.broadcasted_iota(jnp.int32, (8, chans), 0)
    both = jnp.where(row == 0, sums, jnp.where(row == 1, squares, 0.0))
    member = group_matrix(chans, groups)
    fresh = jnp.dot(
        both, member, precision=lax.Precision.HIGHEST, preferred_element_type=jnp.float32
    )
    fresh_ref[...] = fresh[0:2]
    mixed = other_ref[...] + fresh[0:2]
    mean = mixed[0:1] / count
    var = mixed[1:2] / count - mean * mean
    rstd = lax.rsqrt(var + EPS)
    grow = lax.broadcasted_iota(jnp.int32, (8, groups), 0)
    stats = jnp.where(grow == 0, mean, jnp.where(grow == 1, rstd, 0.0))
    wide = lax.dot_general(
        stats,
        member,
        (((1,), (1,)), ((), ())),
        precision=lax.Precision.HIGHEST,
        preferred_element_type=jnp.float32,
    )
    normed = (values - wide[0:1]) * wide[1:2]
    out_ref[...] = (normed * gain_ref[...] + bias_ref[...]).astype(out_ref.dtype)


def normalize(flat, others, gain, bias, count):
    tokens, chans = flat.shape
    groups = others.shape[1]
    return pl.pallas_call(
        functools.partial(norm_kernel, count),
        out_shape=(
            jax.ShapeDtypeStruct((2, groups), jnp.float32),
            jax.ShapeDtypeStruct((tokens, chans), jnp.bfloat16),
        ),
        cost_estimate=pl.CostEstimate(
            flops=8 * tokens * chans, bytes_accessed=4 * tokens * chans, transcendentals=0
        ),
        name="normalize",
    )(flat, others, gain.reshape(1, chans), bias.reshape(1, chans))


def project_kernel(plan, scale, split, *refs):
    ids_ref, left_ref, right_ref = refs[:3]
    pieces = refs[3 : 3 + len(plan)]
    out_ref, held_ref, sem_ref = refs[3 + len(plan) :]
    weights, shards, rows, cols = held_ref.shape
    copies = []
    at = 0
    for piece, offset in zip(pieces, plan):
        for k in range(piece.shape[0]):
            for n in range(weights):
                copies.append(
                    pltpu.make_async_copy(
                        piece.at[k, offset + n],
                        held_ref.at[n, ids_ref[at]],
                        sem_ref.at[len(copies)],
                    )
                )
            at += 1
    for copy in copies:
        copy.start()
    for copy in copies:
        copy.wait()
    for n in range(weights):
        if split:
            tokens = left_ref.shape[1]
            half = shards // 2
            core = ids_ref[at]
            depth = half * rows
            low = held_ref[n, pl.ds(core * half, half)].reshape(depth, cols)
            high = held_ref[n, pl.ds((1 - core) * half, half)].reshape(depth, cols)
            for side in range(2):
                total = jnp.dot(left_ref[side], low, preferred_element_type=jnp.float32)
                total += jnp.dot(
                    right_ref[1 - side], high, preferred_element_type=jnp.float32
                )
                out_ref[n, side] = (total * scale).astype(out_ref.dtype)
        else:
            whole = held_ref[n].reshape(shards * rows, cols)
            for side, ref in enumerate((left_ref, right_ref)):
                total = jnp.dot(ref[...], whole, preferred_element_type=jnp.float32)
                out_ref[n, side] = (total * scale).astype(out_ref.dtype)


def project(left, right, pieces, ids, weights, scale=1.0, split=False):
    tokens = left.shape[-2]
    _, _, rows, cols = pieces[0][0].shape
    shards = sum(piece.shape[0] for piece, _ in pieces)
    depth = shards * rows
    if rows % 16:
        order = jnp.argsort(ids[:shards])
        stacked = jnp.concatenate([p[:, o : o + weights] for p, o in pieces])
        merged = jnp.take(stacked, order, axis=0).transpose(1, 0, 2, 3)
        merged = merged.reshape(weights, 2, depth // 2, cols).transpose(1, 0, 2, 3)
        ids = jnp.concatenate([jnp.arange(2, dtype=jnp.int32), ids[shards:]])
        pieces, shards, rows = [(merged, 0)], 2, depth // 2
    vmem = pl.BlockSpec(memory_space=pltpu.VMEM)
    hbm = pl.BlockSpec(memory_space=pl.ANY)
    return pl.pallas_call(
        functools.partial(project_kernel, tuple(o for _, o in pieces), scale, split),
        out_shape=jax.ShapeDtypeStruct((weights, 2, tokens, cols), jnp.bfloat16),
        in_specs=[pl.BlockSpec(memory_space=pltpu.SMEM), vmem, vmem] + [hbm] * len(pieces),
        out_specs=vmem,
        scratch_shapes=[
            pltpu.VMEM((weights, shards, rows, cols), jnp.bfloat16),
            pltpu.SemaphoreType.DMA((shards * weights,)),
        ],
        cost_estimate=pl.CostEstimate(
            flops=4 * tokens * depth * cols * weights,
            bytes_accessed=2 * weights * (depth * cols + 2 * tokens * cols),
            transcendentals=0,
        ),
        name="project",
    )(ids, left, right, *[p for p, _ in pieces])


def fold(query, keys, vals, low, state):
    ones = jnp.ones_like(vals)
    low_vals = low[: vals.shape[0]]
    out = []
    for head in range(2):
        mine = low if head == 0 else jnp.logical_not(low)
        mine_vals = low_vals if head == 0 else jnp.logical_not(low_vals)
        chosen = jnp.where(mine, query, jnp.zeros_like(query))
        scores = lax.dot_general(
            chosen, keys, (((1,), (1,)), ((), ())), preferred_element_type=jnp.float32
        )
        new_top = jnp.max(scores, axis=-1, keepdims=True)
        if state is not None:
            new_top = jnp.maximum(state[head][0], new_top)
        weights = jnp.exp(scores - new_top).astype(jnp.bfloat16)
        summed = jnp.dot(
            weights, jnp.where(mine_vals, vals, ones), preferred_element_type=jnp.float32
        )
        if state is not None:
            summed += state[head][1] * jnp.exp(state[head][0] - new_top)
        out.append((new_top, summed))
    return out


def attend_kernel(far, carried, final, *refs):
    refs = list(refs)
    refs.pop(0)
    query_ref = refs.pop(0)
    kv_refs = [refs.pop(0), refs.pop(0)]
    if carried:
        top_in, sum_in = refs.pop(0), refs.pop(0)
    tokens = query_ref.shape[1]
    low = lax.broadcasted_iota(jnp.int32, (tokens, PAIR), 1) < HEAD
    for side in range(2):
        query = query_ref[side]
        state = None
        if carried:
            tops = top_in[side]
            state = [
                (tops[:, 0:1], sum_in[side, :, :PAIR]),
                (tops[:, HEAD : HEAD + 1], sum_in[side, :, PAIR:]),
            ]
        for at, ref in enumerate(kv_refs):
            if far or at == side:
                state = fold(query, ref[0], ref[1], low, state)
        (top_a, sum_a), (top_b, sum_b) = state
        if final:
            total = jnp.where(low, pltpu.roll(sum_a, HEAD, 1), pltpu.roll(sum_b, HEAD, 1))
            refs[0][side] = (jnp.where(low, sum_a, sum_b) / total).astype(refs[0].dtype)
        else:
            refs[0][side] = jnp.where(low, top_a, top_b)
            refs[1][side, :, :PAIR] = sum_a
            refs[1][side, :, PAIR:] = sum_b


def attend(core, query, kv, carry=None, far=False, final=False, name="attend"):
    _, tokens, cols = query.shape
    pairs = cols // PAIR
    wide = pl.BlockSpec((2, tokens, PAIR), lambda p, c: (0, 0, p))
    own = pl.BlockSpec((2, tokens, PAIR), lambda p, c: (0, 0, c[0] * pairs + p))
    double = pl.BlockSpec((2, tokens, 2 * PAIR), lambda p, c: (0, 0, p))
    in_specs = [wide] + [wide if a.shape[2] == cols else own for a in kv]
    args = [query, *kv]
    if carry is not None:
        in_specs += [wide, double]
        args += list(carry)
    if final:
        out_shape = jax.ShapeDtypeStruct((2, tokens, cols), jnp.bfloat16)
        out_specs = wide
    else:
        out_shape = (
            jax.ShapeDtypeStruct((2, tokens, cols), jnp.float32),
            jax.ShapeDtypeStruct((2, tokens, 2 * cols), jnp.float32),
        )
        out_specs = (wide, double)
    blocks = 4 if far else 2
    return pl.pallas_call(
        functools.partial(attend_kernel, far, carry is not None, final),
        grid_spec=pltpu.PrefetchScalarGridSpec(
            num_scalar_prefetch=1, grid=(pairs,), in_specs=in_specs, out_specs=out_specs
        ),
        out_shape=out_shape,
        cost_estimate=pl.CostEstimate(
            flops=blocks * tokens * tokens * cols * 16,
            bytes_accessed=40 * tokens * cols,
            transcendentals=blocks * tokens * tokens * cols // HEAD,
        ),
        name=name,
    )(core, *args)


def line_stages(nodes):
    stages = []
    span = 1
    while span < nodes:
        hops = [[] for _ in range(span)]
        place = [0] * nodes
        giver = [0] * nodes
        for base in range(0, nodes, 2 * span):
            middle = base + span
            for hop in range(span):
                below, above = middle - 1 - hop, middle + hop
                place[below] = place[above] = hop
                giver[below], giver[above] = middle, middle - 1
                if hop == 0:
                    hops[0] += [(above, below), (below, above)]
                else:
                    hops[hop] += [(below + 1, below), (above - 1, above)]
        stages.append((hops, place, giver))
        span *= 2
    return stages


class Rows:
    def __init__(self):
        self.count = lax.axis_size("rows")
        self.line = self.count // 2
        index = lax.axis_index("rows")
        self.node, self.side = index // 2, index % 2
        self.stages = line_stages(self.line)

    def across(self, value, name):
        with jax.named_scope(name):
            return lax.ppermute(value, "rows", [(i, i ^ 1) for i in range(self.count)])

    def along(self, value, name):
        pieces = [value]
        for at, (hops, place, _) in enumerate(self.stages):
            payload = pieces[0] if len(pieces) == 1 else jnp.concatenate(pieces)
            moved = payload
            chosen = None
            for hop, pairs in enumerate(hops):
                with jax.named_scope(f"{name}{at}{hop}"):
                    moved = lax.ppermute(
                        moved, "rows", [(2 * a + s, 2 * b + s) for a, b in pairs for s in (0, 1)]
                    )
                here = jnp.asarray(place, jnp.int32)[self.node] == hop
                chosen = moved if chosen is None else jnp.where(here, moved, chosen)
            pieces.append(chosen)
        return pieces

    def nodes(self):
        held = [[n] for n in range(self.line)]
        for _, _, giver in self.stages:
            held = [held[n] + held[giver[n]] for n in range(self.line)]
        return jnp.asarray(held, jnp.int32)[self.node]


def shards(tokens, stale_kv, stale_moments, norm_gain, norm_bias, w_query, w_key, w_value, w_out):
    _, band, width, chans = tokens.shape
    tok_count = band * width
    groups = stale_moments.shape[3]
    strips = lax.axis_size("strips")
    core = lax.axis_index("strips") % 2
    core_ids = core.astype(jnp.int32).reshape(1)
    half = w_query.shape[1] // 2
    rows = Rows()

    def swap(value, bits, name):
        with jax.named_scope(name):
            return lax.ppermute(value, "strips", [(i, i ^ bits) for i in range(strips)])

    def half_of(value, which):
        return lax.dynamic_slice_in_dim(value, which * half, half, value.ndim - 1)

    own_kv = stale_kv[0]
    own_moments = stale_moments[0, 0]
    near_moments = swap(own_moments, 1, "moments_near")
    far_moments = swap(own_moments + near_moments, 2, "moments_far")

    own_q = half_of(w_query, core)[None, None]
    own_kvw = jnp.stack([half_of(w_key, core), half_of(w_value, core)])[None]
    own_o = half_of(w_out, core)[None, None]
    cross_q = rows.across(own_q, "q_cross")
    q_parts = rows.along(own_q, "q_line")
    cross_kv = rows.across(own_kvw, "kv_cross")
    kv_parts = rows.along(own_kvw, "kv_line")
    cross_o = rows.across(own_o, "o_cross")
    o_parts = rows.along(jnp.concatenate([own_o, cross_o]), "o_line")
    q_other = [cross_q] + [rows.across(p, f"q_over{i}") for i, p in enumerate(q_parts[1:])]
    kv_other = [cross_kv] + [rows.across(p, f"kv_over{i}") for i, p in enumerate(kv_parts[1:])]
    nodes = rows.nodes()
    ids = jnp.concatenate([nodes * 2 + rows.side, nodes * 2 + 1 - rows.side])

    stale_other = half_of(own_kv, 1 - core)
    stale_mine = half_of(own_kv, core)
    near_kv = swap(stale_other, 1, "stale_near")
    far_kv = swap(stale_mine, 2, "stale_far")
    diag_kv = swap(stale_other, 3, "stale_diag")

    flat = tokens.reshape(tok_count, chans)
    count = float(tok_count * strips * (chans // groups))
    fresh, normed = normalize(flat, near_moments + far_moments, norm_gain, norm_bias, count)
    normed_pair = swap(normed, 1, "normed_near")

    query = project(
        normed, normed_pair, [(p, 0) for p in q_parts + q_other], ids, 1, 1.0 / HEAD**0.5
    )[0]
    carry = attend(core_ids, query, [near_kv, own_kv], name="attend_near")
    carry = attend(core_ids, query, [far_kv, diag_kv], carry, far=True, name="attend_far")
    kv = project(normed, normed_pair, [(p, 0) for p in kv_parts + kv_other], ids, 2)
    kv_mine, kv_sent = kv[:, 0], kv[:, 1]
    kv_back = swap(kv_sent, 1, "fresh_near")
    heads = attend(core_ids, query, [kv_mine, kv_sent], carry, final=True, name="attend_fresh")
    heads_pair = swap(heads, 1, "heads_near")

    pair_ids = jnp.stack([rows.side, 1 - rows.side])
    o_ids = (nodes[:, None] * 2 + pair_ids[None, :]).reshape(-1)
    order = []
    at = 0
    for p in o_parts:
        order.append(o_ids[at : at + p.shape[0]])
        at += p.shape[0]
    out = project(
        heads,
        heads_pair,
        [(p, 0) for p in o_parts],
        jnp.concatenate(order + [core_ids]),
        1,
        split=True,
    )[0]
    out_back = swap(out[1], 1, "out_near")

    def joined(mine, other):
        wide = jnp.zeros(mine.shape[:-1] + (2 * half,), mine.dtype)
        first = jnp.where(core == 0, mine, other)
        second = jnp.where(core == 0, other, mine)
        del wide
        return jnp.concatenate([first, second], axis=-1)

    attended = joined(out[0], out_back)
    fresh_kv = joined(kv_mine, kv_back)
    return (
        attended.reshape(1, band, width, chans),
        fresh_kv[None],
        fresh[0][None, None],
        fresh[1][None, None],
    )


def solution(mesh):
    in_specs = (
        P("rows", None, "strips", None),
        P("rows", None, "strips", None),
        P("rows", "strips", None, None),
        P(),
        P(),
        P("rows", None),
        P("rows", None),
        P("rows", None),
        P("rows", None),
    )
    out_specs = (
        P("rows", None, "strips", None),
        P("rows", None, "strips", None),
        P("rows", "strips", None),
        P("rows", "strips", None),
    )
    return jax.shard_map(shards, mesh=mesh, in_specs=in_specs, out_specs=out_specs, check_vma=False)
```

```python
import functools

import jax
import jax.numpy as jnp
from jax import lax
from jax.experimental import pallas as pl
from jax.experimental.pallas import tpu as pltpu
from jax.sharding import PartitionSpec as P


HEAD = 64
PAIR = 2 * HEAD
EPS = 1e-05


def group_matrix(chans, groups):
    per = chans // groups
    first = lax.broadcasted_iota(jnp.int32, (chans, groups), 1) * per
    place = lax.broadcasted_iota(jnp.int32, (chans, groups), 0)
    return jnp.where((place >= first) & (place < first + per), 1.0, 0.0).astype(jnp.bfloat16)


def exact_dot(rows, member, dims):
    high = rows.astype(jnp.bfloat16)
    rest = rows - high.astype(jnp.float32)
    middle = rest.astype(jnp.bfloat16)
    low = (rest - middle.astype(jnp.float32)).astype(jnp.bfloat16)
    parts = [
        lax.dot_general(p, member, (dims, ((), ())), preferred_element_type=jnp.float32)
        for p in (high, middle, low)
    ]
    return (parts[2] + parts[1]) + parts[0]


def norm_kernel(count, tok_ref, other_ref, gain_ref, bias_ref, fresh_ref, out_ref):
    chans = tok_ref.shape[1]
    groups = fresh_ref.shape[1]
    values = tok_ref[...].astype(jnp.float32)
    sums = jnp.sum(values, axis=0, keepdims=True)
    squares = jnp.sum(values * values, axis=0, keepdims=True)
    row = lax.broadcasted_iota(jnp.int32, (8, chans), 0)
    both = jnp.where(row == 0, sums, jnp.where(row == 1, squares, 0.0))
    member = group_matrix(chans, groups)
    fresh = exact_dot(both, member, ((1,), (0,)))
    fresh_ref[...] = fresh[0:2]
    mixed = other_ref[...] + fresh[0:2]
    mean = mixed[0:1] / count
    var = mixed[1:2] / count - mean * mean
    rstd = lax.rsqrt(var + EPS)
    grow = lax.broadcasted_iota(jnp.int32, (8, groups), 0)
    stats = jnp.where(grow == 0, mean, jnp.where(grow == 1, rstd, 0.0))
    wide = exact_dot(stats, member, ((1,), (1,)))
    normed = (values - wide[0:1]) * wide[1:2]
    gain = gain_ref[...].reshape(1, chans)
    bias = bias_ref[...].reshape(1, chans)
    out_ref[...] = (normed * gain + bias).astype(out_ref.dtype)


def normalize(flat, others, gain, bias, count):
    tokens, chans = flat.shape
    groups = others.shape[1]
    return pl.pallas_call(
        functools.partial(norm_kernel, count),
        out_shape=(
            jax.ShapeDtypeStruct((2, groups), jnp.float32),
            jax.ShapeDtypeStruct((tokens, chans), jnp.bfloat16),
        ),
        cost_estimate=pl.CostEstimate(
            flops=8 * tokens * chans, bytes_accessed=4 * tokens * chans, transcendentals=0
        ),
        compiler_params=pltpu.CompilerParams(vmem_limit_bytes=12 << 20),
        name="normalize",
    )(flat, others, gain, bias)


def project_kernel(plan, scale, split, *refs):
    ids_ref, left_ref, right_ref = refs[:3]
    pieces = refs[3 : 3 + len(plan)]
    mine_ref, sent_ref, tokens_ref, held_ref, sem_ref = refs[3 + len(plan) :]
    shards, rows, cols = held_ref.shape
    copies = [
        pltpu.make_async_copy(left_ref, tokens_ref.at[0], sem_ref.at[0]),
        pltpu.make_async_copy(right_ref, tokens_ref.at[1], sem_ref.at[1]),
    ]
    at = 0
    for piece, offset in zip(pieces, plan):
        for k in range(piece.shape[0]):
            copies.append(
                pltpu.make_async_copy(
                    piece.at[k, offset], held_ref.at[ids_ref[at]], sem_ref.at[2 + at]
                )
            )
            at += 1

    @pl.when(pl.program_id(0) == 0)
    def _():
        for copy in copies:
            copy.start()
        for copy in copies:
            copy.wait()

    def compute(side, out_ref):
        if split:
            half = shards // 2
            core = ids_ref[at]
            depth = half * rows
            low = held_ref[pl.ds(core * half, half)].reshape(depth, cols)
            high = held_ref[pl.ds((1 - core) * half, half)].reshape(depth, cols)
            total = jnp.dot(tokens_ref[0, side], low, preferred_element_type=jnp.float32)
            total += jnp.dot(tokens_ref[1, 1 - side], high, preferred_element_type=jnp.float32)
        else:
            whole = held_ref[...].reshape(shards * rows, cols)
            total = jnp.dot(tokens_ref[side], whole, preferred_element_type=jnp.float32)
        out_ref[...] = (total * scale).astype(out_ref.dtype)

    @pl.when(pl.program_id(0) == 0)
    def _():
        compute(1, sent_ref)

    @pl.when(pl.program_id(0) == 1)
    def _():
        compute(0, mine_ref)


def project(left, right, pieces, ids, scale=1.0, split=False):
    tokens = left.shape[-2]
    _, _, rows, cols = pieces[0][0].shape
    shards = sum(piece.shape[0] for piece, _ in pieces)
    depth = shards * rows
    if rows % 16:
        order = jnp.argsort(ids[:shards])
        stacked = jnp.concatenate([p[:, o : o + 1] for p, o in pieces])
        merged = jnp.take(stacked, order, axis=0).reshape(2, 1, depth // 2, cols)
        ids = jnp.concatenate([jnp.arange(2, dtype=jnp.int32), ids[shards:]])
        pieces, shards, rows = [(merged, 0)], 2, depth // 2
    hbm = pl.BlockSpec(memory_space=pl.ANY)
    out = jax.ShapeDtypeStruct((tokens, cols), jnp.bfloat16)
    whole = pl.BlockSpec((tokens, cols), lambda i: (0, 0))
    return pl.pallas_call(
        functools.partial(project_kernel, tuple(o for _, o in pieces), scale, split),
        grid=(2,),
        out_shape=(out, out),
        in_specs=[pl.BlockSpec(memory_space=pltpu.SMEM)] + [hbm] * (2 + len(pieces)),
        out_specs=(whole, whole),
        scratch_shapes=[
            pltpu.VMEM((2, *left.shape), jnp.bfloat16),
            pltpu.VMEM((shards, rows, cols), jnp.bfloat16),
            pltpu.SemaphoreType.DMA((shards + 2,)),
        ],
        cost_estimate=pl.CostEstimate(
            flops=4 * tokens * depth * cols,
            bytes_accessed=2 * (depth * cols + 4 * tokens * cols),
            transcendentals=0,
        ),
        compiler_params=pltpu.CompilerParams(vmem_limit_bytes=12 << 20),
    )(ids, left, right, *[p for p, _ in pieces])


def both_heads(query, keys, vals):
    tokens = query.shape[0]
    low = lax.broadcasted_iota(jnp.int32, (tokens, PAIR), 1) < HEAD
    zero = jnp.zeros_like(query)
    stacked = jnp.concatenate([jnp.where(low, query, zero), jnp.where(low, zero, query)])
    scores = lax.dot_general(
        stacked, keys, (((1,), (1,)), ((), ())), preferred_element_type=jnp.float32
    )
    top = jnp.max(scores, axis=-1, keepdims=True)
    weights = jnp.exp(scores - top).astype(jnp.bfloat16)
    summed = jnp.dot(
        weights,
        jnp.concatenate([vals, jnp.ones_like(vals)], axis=1),
        preferred_element_type=jnp.float32,
    )
    return (
        jnp.where(low, top[:tokens], top[tokens:]),
        jnp.where(low, summed[:tokens, :PAIR], summed[tokens:, :PAIR]),
        jnp.where(low, summed[:tokens, PAIR:], summed[tokens:, PAIR:]),
    )


def stale_kernel(
    core_ref, q0_ref, q1_ref, near_ref, own_ref, far_ref, diag_ref, top_ref, sum_ref, total_ref
):
    for side, (q_ref, first) in enumerate(((q0_ref, near_ref), (q1_ref, own_ref))):
        keys = jnp.concatenate([first[0], far_ref[0], diag_ref[0]])
        vals = jnp.concatenate([first[1], far_ref[1], diag_ref[1]])
        top_ref[side], sum_ref[side], total_ref[side] = both_heads(q_ref[...], keys, vals)


def fresh_kernel(
    q0_ref, q1_ref, k0_ref, k1_ref, v0_ref, v1_ref, top_ref, sum_ref, total_ref, out_ref
):
    for side, (q_ref, k_ref, v_ref) in enumerate(
        ((q0_ref, k0_ref, v0_ref), (q1_ref, k1_ref, v1_ref))
    ):
        here, summed, total = both_heads(q_ref[...], k_ref[...], v_ref[...])
        before = top_ref[side]
        top = jnp.maximum(here, before)
        new, old = jnp.exp(here - top), jnp.exp(before - top)
        summed = summed * new + sum_ref[side] * old
        total = total * new + total_ref[side] * old
        out_ref[side] = (summed / total).astype(out_ref.dtype)


def attend_stale(core, queries, near, own, far, diag):
    tokens, cols = queries[0].shape
    pairs = cols // PAIR
    flat = pl.BlockSpec((tokens, PAIR), lambda p, c: (0, p))
    wide = pl.BlockSpec((2, tokens, PAIR), lambda p, c: (0, 0, p))
    mine = pl.BlockSpec((2, tokens, PAIR), lambda p, c: (0, 0, c[0] * pairs + p))
    return pl.pallas_call(
        stale_kernel,
        grid_spec=pltpu.PrefetchScalarGridSpec(
            num_scalar_prefetch=1,
            grid=(pairs,),
            in_specs=[flat, flat, wide, mine, wide, wide],
            out_specs=(wide,) * 3,
        ),
        out_shape=(jax.ShapeDtypeStruct((2, tokens, cols), jnp.float32),) * 3,
        cost_estimate=pl.CostEstimate(
            flops=6 * tokens * tokens * cols * 16,
            bytes_accessed=40 * tokens * cols,
            transcendentals=6 * tokens * tokens * cols // HEAD,
        ),
        compiler_params=pltpu.CompilerParams(vmem_limit_bytes=20 << 20),
        name="attend_stale",
    )(core, *queries, near, own, far, diag)


def attend_fresh(queries, keys, vals, carry):
    tokens, cols = queries[0].shape
    pairs = cols // PAIR
    flat = pl.BlockSpec((tokens, PAIR), lambda p: (0, p))
    wide = pl.BlockSpec((2, tokens, PAIR), lambda p: (0, 0, p))
    return pl.pallas_call(
        fresh_kernel,
        grid=(pairs,),
        in_specs=[flat] * 6 + [wide] * 3,
        out_specs=wide,
        out_shape=jax.ShapeDtypeStruct((2, tokens, cols), jnp.bfloat16),
        cost_estimate=pl.CostEstimate(
            flops=2 * tokens * tokens * cols * 16,
            bytes_accessed=40 * tokens * cols,
            transcendentals=2 * tokens * tokens * cols // HEAD,
        ),
        compiler_params=pltpu.CompilerParams(vmem_limit_bytes=12 << 20),
        name="attend_fresh",
    )(*queries, *keys, *vals, *carry)


def join_kernel(core_ref, mine_ref, other_ref, out_ref):
    own = pl.program_id(0) == core_ref[0]

    @pl.when(own)
    def _():
        out_ref[...] = mine_ref[...]

    @pl.when(jnp.logical_not(own))
    def _():
        out_ref[...] = other_ref[...]


def join(core, mine, other):
    tokens, cols = mine.shape
    whole = pl.BlockSpec((tokens, cols), lambda j, c: (0, 0))
    return pl.pallas_call(
        join_kernel,
        grid_spec=pltpu.PrefetchScalarGridSpec(
            num_scalar_prefetch=1,
            grid=(2,),
            in_specs=[whole, whole],
            out_specs=pl.BlockSpec((tokens, cols), lambda j, c: (0, j)),
        ),
        out_shape=jax.ShapeDtypeStruct((tokens, 2 * cols), mine.dtype),
        cost_estimate=pl.CostEstimate(
            flops=0, bytes_accessed=8 * tokens * cols, transcendentals=0
        ),
        compiler_params=pltpu.CompilerParams(vmem_limit_bytes=6 << 20),
    )(core, mine, other)


def join_kv_kernel(core_ref, *refs):
    own = pl.program_id(0) == core_ref[0]
    out_ref = refs[-1]

    @pl.when(own)
    def _():
        out_ref[0] = refs[0][...]
        out_ref[1] = refs[1][...]

    @pl.when(jnp.logical_not(own))
    def _():
        out_ref[0] = refs[2][...]
        out_ref[1] = refs[3][...]


def join_kv(core, key, value, other_key, other_value):
    tokens, cols = key.shape
    whole = pl.BlockSpec((tokens, cols), lambda j, c: (0, 0))
    return pl.pallas_call(
        join_kv_kernel,
        grid_spec=pltpu.PrefetchScalarGridSpec(
            num_scalar_prefetch=1,
            grid=(2,),
            in_specs=[whole] * 4,
            out_specs=pl.BlockSpec((2, tokens, cols), lambda j, c: (0, 0, j)),
        ),
        out_shape=jax.ShapeDtypeStruct((2, tokens, 2 * cols), key.dtype),
        cost_estimate=pl.CostEstimate(
            flops=0, bytes_accessed=16 * tokens * cols, transcendentals=0
        ),
        compiler_params=pltpu.CompilerParams(vmem_limit_bytes=8 << 20),
        name="join_kv",
    )(core, key, value, other_key, other_value)


def line_stages(nodes):
    stages = []
    span = 1
    while span < nodes:
        hops = [[] for _ in range(span)]
        place = [0] * nodes
        giver = [0] * nodes
        for base in range(0, nodes, 2 * span):
            middle = base + span
            for hop in range(span):
                below, above = middle - 1 - hop, middle + hop
                place[below] = place[above] = hop
                giver[below], giver[above] = middle, middle - 1
                if hop == 0:
                    hops[0] += [(above, below), (below, above)]
                else:
                    hops[hop] += [(below + 1, below), (above - 1, above)]
        stages.append((hops, place, giver))
        span *= 2
    return stages


class Rows:
    def __init__(self):
        self.count = lax.axis_size("rows")
        self.line = self.count // 2
        index = lax.axis_index("rows")
        self.node, self.side = index // 2, index % 2
        self.stages = line_stages(self.line)

    def across(self, value):
        return lax.ppermute(value, "rows", [(i, i ^ 1) for i in range(self.count)])

    def along(self, at, value):
        hops, place, _ = self.stages[at]
        chosen = None
        for hop, pairs in enumerate(hops):
            value = lax.ppermute(
                value, "rows", [(2 * a + s, 2 * b + s) for a, b in pairs for s in (0, 1)]
            )
            here = jnp.asarray(place, jnp.int32)[self.node] == hop
            chosen = value if chosen is None else jnp.where(here, value, chosen)
        return chosen

    def rest(self, pieces):
        found = []
        for at in range(1, len(self.stages)):
            found.append(self.along(at, jnp.concatenate(pieces)))
            pieces = pieces + [found[-1]]
        return found

    def nodes(self):
        held = [[n] for n in range(self.line)]
        for _, _, giver in self.stages:
            held = [held[n] + held[giver[n]] for n in range(self.line)]
        return jnp.asarray(held, jnp.int32)[self.node]


def block(tokens, stale_kv, stale_moments, norm_gain, norm_bias, w_query, w_key, w_value, w_out):
    _, band, width, chans = tokens.shape
    tok_count = band * width
    groups = stale_moments.shape[3]
    strips = lax.axis_size("strips")
    core = lax.axis_index("strips") % 2
    core_ids = core.astype(jnp.int32).reshape(1)
    half = w_query.shape[1] // 2
    rows = Rows()

    def swap(value, bits):
        return lax.ppermute(value, "strips", [(i, i ^ bits) for i in range(strips)])

    def half_of(value, which):
        return lax.dynamic_slice_in_dim(value, which * half, half, value.ndim - 1)

    own = {n: half_of(w, core)[None, None] for n, w in zip("qkvo", (w_query, w_key, w_value, w_out))}
    own_kv = jnp.concatenate([own["k"], own["v"]], axis=1)
    own_kvo = jnp.concatenate([own["k"], own["v"], own["o"]], axis=1)
    next_q = rows.along(0, own["q"])
    next_kvo = rows.along(0, own_kvo)
    next_of = {"q": next_q, **{n: next_kvo[:, i : i + 1] for i, n in enumerate("kvo")}}
    cross_q = rows.across(own["q"])
    cross_kv = rows.across(own_kv)
    cross_o = rows.across(own["o"])
    cross_of = {"q": (cross_q, 0), "k": (cross_kv, 0), "v": (cross_kv, 1), "o": (cross_o, 0)}
    pieces = {}
    for n in "qkvo":
        rest = rows.rest([own[n], next_of[n]])
        over = [rows.across(p) for p in [next_of[n], *rest]]
        at = "kvo".index(n) if n != "q" else 0
        pieces[n] = [(own[n], 0), (next_q if n == "q" else next_kvo, at)]
        pieces[n] += [(p, 0) for p in rest] + [cross_of[n]] + [(p, 0) for p in over]
    nodes = rows.nodes()
    ids = jnp.concatenate([nodes * 2 + rows.side, nodes * 2 + 1 - rows.side, core_ids])

    own_stale = stale_kv[0]
    own_moments = stale_moments[0, 0]
    near_moments = swap(own_moments, 1)
    far_moments = swap(own_moments + near_moments, 2)
    stale_other = half_of(own_stale, 1 - core)
    far_stale = swap(half_of(own_stale, core), 2)
    diag_stale = swap(stale_other, 3)
    near_stale = swap(stale_other, 1)

    flat = tokens.reshape(tok_count, chans)
    count = float(tok_count * strips * (chans // groups))
    fresh, normed = normalize(flat, near_moments + far_moments, norm_gain, norm_bias, count)
    normed_pair = swap(normed, 1)

    query = project(normed, normed_pair, pieces["q"], ids, 1.0 / HEAD**0.5)
    carry = attend_stale(core_ids, query, near_stale, own_stale, far_stale, diag_stale)
    key = project(normed, normed_pair, pieces["k"], ids)
    value = project(normed, normed_pair, pieces["v"], ids)
    other_key = swap(key[1], 1)
    other_value = swap(value[1], 1)
    heads = attend_fresh(query, key, value, carry)
    heads_pair = swap(heads, 1)
    fresh_kv = join_kv(core_ids, key[0], value[0], other_key, other_value)
    out = project(heads, heads_pair, pieces["o"], ids, split=True)
    attended = join(core_ids, out[0], swap(out[1], 1))
    return (
        attended.reshape(1, band, width, chans),
        fresh_kv[None],
        fresh[0][None, None],
        fresh[1][None, None],
    )


def solution(mesh):
    in_specs = (
        P("rows", None, "strips", None),
        P("rows", None, "strips", None),
        P("rows", "strips", None, None),
        P(),
        P(),
        P("rows", None),
        P("rows", None),
        P("rows", None),
        P("rows", None),
    )
    out_specs = (
        P("rows", None, "strips", None),
        P("rows", None, "strips", None),
        P("rows", "strips", None),
        P("rows", "strips", None),
    )
    return jax.shard_map(block, mesh=mesh, in_specs=in_specs, out_specs=out_specs, check_vma=False)
```
